32 devices in a mesh: section: 4 (over x, core), expert: 8 (over z, y).
Axes of the slice: x: 2, y: 2, z: 4, core: 2. Of those that a mesh axis runs over, the one named last changes fastest.
Arguments:
- tokens: bfloat16 [4, 512, 4096], P('section', 'expert'), may hold values from -6 to 6
- out_grad: bfloat16 [4, 512, 4096], P('section', 'expert'), may hold values from -6 to 6
- expert_ids: int32 [4, 512, 2], P('section', 'expert'), may hold values from 0 to 7, as said below
- slot_ids: int32 [4, 512, 2], P('section', 'expert'), may hold values from 0 to 15, as said below
- gate_int: int32 [4, 512, 2], P('section', 'expert'), may hold values from 16 to 255
- saved_gate: bfloat16 [4, 128, 14336], P('section', None, 'expert'), may hold values from -6 to 6
- saved_up: bfloat16 [4, 128, 14336], P('section', None, 'expert'), may hold values from -6 to 6
- w_gate: bfloat16 [4, 4096, 14336], P('section', None, 'expert'), may hold values from -0.09375 to 0.09375
- w_up: bfloat16 [4, 4096, 14336], P('section', None, 'expert'), may hold values from -0.09375 to 0.09375
- w_down: bfloat16 [4, 14336, 4096], P('section', 'expert'), may hold values from -0.0625 to 0.0625
Outputs:
- arriving_grad: bfloat16 [4, 512, 4096], P('section', 'expert')
- grad_w_gate: bfloat16 [4, 4096, 14336], P('section', None, 'expert')
- grad_w_up: bfloat16 [4, 4096, 14336], P('section', None, 'expert')
- grad_w_down: bfloat16 [4, 14336, 4096], P('section', 'expert')
The draws below stay inside these ranges and needn't reach their ends.
Inputs may be any that keep to these rules, and one draw needn't show every extreme that they name: `expert_ids`: in each section, the 64 tokens of each index of expert name each of the 8 experts exactly 16 times; a token's two experts differ. `slot_ids`: for each expert, the slots of the 64 tokens of one index of expert that name it are 0 to 15, each once.
All inputs are finite; a program needn't handle non-finite values.
Results may differ from the reference program's by a relative error of at most 0.018.
Values may be sent and summed in bfloat16 or wider, within the bound.
No kernel may reach another device: no remote copies, remote signals or barrier semaphores. Data moves between devices by JAX's collectives and lax.ppermute only.
A program may use at most 128 MiB of HBM per device.

```python
import jax
import jax.numpy as jnp
from jax import lax

D = 4096
EXPERTS = 8
H_WIN = 7168
E_WIN = 2
TOK_DEV = 64
CAP = 16
TOKENS = 512
SECTIONS = 4
N_EXPERT = 8


def routing_tables(key):
    blocks = SECTIONS * (TOKENS // TOK_DEV)

    def one_block(block_key):
        rank_key, label_key, slot_key = jax.random.split(block_key, 3)
        token_rank = jax.random.permutation(rank_key, TOK_DEV).astype(jnp.int32)
        relabel = jax.random.permutation(label_key, EXPERTS).astype(jnp.int32)
        slot_perms = jax.vmap(lambda one_key: jax.random.permutation(one_key, CAP).astype(jnp.int32))(jax.random.split(slot_key, EXPERTS))
        lane_index = token_rank % EXPERTS
        rounds = token_rank // EXPERTS
        second = (lane_index + 1 + rounds % (EXPERTS - 1)) % EXPERTS
        chosen = jnp.stack([relabel[lane_index], relabel[second]], axis=-1)
        first_slot = slot_perms[lane_index, rounds]
        second_slot = slot_perms[second, TOK_DEV // EXPERTS + rounds]
        places = jnp.stack([first_slot, second_slot], axis=-1)
        return (chosen, places)
    chosen, places = jax.vmap(one_block)(jax.random.split(key, blocks))
    return (chosen.reshape(SECTIONS, TOKENS, 2).astype(jnp.int32), places.reshape(SECTIONS, TOKENS, 2).astype(jnp.int32))


def draw_expert_ids(key, part):
    return routing_tables(jax.random.fold_in(key, 17))[0]


def draw_slot_ids(key, part):
    return routing_tables(jax.random.fold_in(key, 17))[1]


def plant(array, key, smallest, largest):
    shape = array.shape
    index_at = [jax.random.randint(jax.random.fold_in(key, axis), (), 0, shape[axis]) for axis in range(len(shape))]
    array = array.at[tuple(index_at)].set(smallest)
    longest = shape.index(max(shape))
    index_at[longest] = (index_at[longest] + 1) % shape[longest]
    return array.at[tuple(index_at)].set(largest)


def levels(key, extent, pieces, smallest, largest):
    def one(dim, shards_of):
        steps = jax.random.uniform(jax.random.fold_in(jax.random.fold_in(key, 6), dim), (shards_of,), jnp.float32, smallest / len(pieces), largest / len(pieces))
        return jnp.repeat(jnp.exp(steps), extent[dim] // shards_of).reshape((-1,) + (1,) * (len(extent) - dim - 1))

    gain = one(*pieces[0])
    for cut in pieces[1:]:
        gain = gain * one(*cut)
    return gain


def bell_draw(key, dims, width, reach, pieces=(), held_as=jnp.bfloat16):
    values = width * jax.random.normal(key, dims, jnp.float32)
    if pieces:
        values = values * levels(key, dims, pieces, -0.22, 0.18)
    return jnp.clip(values, -reach, reach).astype(held_as)


def setup_inputs(seed: int = 0) -> dict:
    streams_of = jax.random.split(jax.random.key(seed), 11)
    tokens = bell_draw(streams_of[0], (SECTIONS, TOKENS, D), 1.0, 6.0, ((0, 4), (1, 8)))
    out_grad = bell_draw(streams_of[1], (SECTIONS, TOKENS, D), 1.0, 6.0, ((0, 4), (1, 8)))
    expert_ids = draw_expert_ids(jax.random.fold_in(streams_of[10], 71), 0)
    slot_ids = draw_slot_ids(jax.random.fold_in(streams_of[10], 71), 0)
    gate_int = plant(jax.random.randint(streams_of[4], (SECTIONS, TOKENS, 2), 16, 256), jax.random.fold_in(streams_of[4], 1), 16, 255).astype(jnp.int32)
    saved_gate = bell_draw(streams_of[5], (SECTIONS, N_EXPERT * CAP, E_WIN * H_WIN), 1.5, 6.0, ((0, 4), (2, 8)))
    saved_up = bell_draw(streams_of[6], (SECTIONS, N_EXPERT * CAP, E_WIN * H_WIN), 1.0, 6.0, ((0, 4), (2, 8)))
    w_gate = bell_draw(streams_of[7], (SECTIONS, D, E_WIN * H_WIN), D ** -0.5, 0.09375, ((0, 4), (2, 8)))
    w_up = bell_draw(streams_of[8], (SECTIONS, D, E_WIN * H_WIN), D ** -0.5, 0.09375, ((0, 4), (2, 8)))
    w_down = bell_draw(streams_of[9], (SECTIONS, E_WIN * H_WIN, D), H_WIN ** -0.5, 0.0625, ((0, 4), (1, 8)))
    return {"tokens": tokens, "out_grad": out_grad, "expert_ids": expert_ids, "slot_ids": slot_ids, "gate_int": gate_int, "saved_gate": saved_gate, "saved_up": saved_up, "w_gate": w_gate, "w_up": w_up, "w_down": w_down}


def section_grads(inputs, upstream_grad, chosen, places, gate_int, saved_gate, saved_up, w_gate, w_up, w_down):
    per_expert = N_EXPERT // E_WIN
    shard_width = H_WIN // per_expert
    row_total = N_EXPERT * CAP
    block_of = (jnp.arange(TOKENS, dtype=jnp.int32) // TOK_DEV)[:, None]
    weights_k = gate_int.astype(jnp.float32) / 256.0
    gated = (upstream_grad.astype(jnp.float32)[:, None, :] * weights_k[:, :, None]).astype(jnp.bfloat16)
    repeated = jnp.broadcast_to(inputs[:, None, :], (TOKENS, 2, D))
    result = jnp.zeros((TOKENS, D), jnp.float32)
    grads_gate = []
    grads_up = []
    grads_down = []
    for expert_num in range(E_WIN):
        hit = chosen == expert_num
        target = jnp.where(hit, block_of * CAP + places, row_total).astype(jnp.int32)
        flat_rows = target.reshape(-1)
        rows_in = jnp.zeros((row_total, D), jnp.bfloat16).at[flat_rows].set(repeated.reshape(-1, D), mode="drop")
        rows_grad = jnp.zeros((row_total, D), jnp.bfloat16).at[flat_rows].set(gated.reshape(-1, D), mode="drop")
        first = expert_num * H_WIN
        gate_pre = saved_gate[:, first:first + H_WIN].astype(jnp.float32)
        up_pre = saved_up[:, first:first + H_WIN].astype(jnp.float32)
        sigmoid_g = jax.nn.sigmoid(gate_pre)
        activated = gate_pre * sigmoid_g
        hidden = (activated * up_pre).astype(jnp.bfloat16)
        hidden_grad = jnp.dot(rows_grad, w_down[first:first + H_WIN, :].T, preferred_element_type=jnp.float32)
        gate_grad = (hidden_grad * up_pre * sigmoid_g * (1.0 + gate_pre * (1.0 - sigmoid_g))).astype(jnp.bfloat16)
        up_grad = (hidden_grad * activated).astype(jnp.bfloat16)
        grads_down.append(jnp.dot(hidden.T, rows_grad, preferred_element_type=jnp.float32).astype(jnp.bfloat16))
        grads_gate.append(jnp.dot(rows_in.T, gate_grad, preferred_element_type=jnp.float32).astype(jnp.bfloat16))
        grads_up.append(jnp.dot(rows_in.T, up_grad, preferred_element_type=jnp.float32).astype(jnp.bfloat16))
        gate_parts = jnp.einsum("rgh,dgh->grd", gate_grad.astype(jnp.float32).reshape(row_total, per_expert, shard_width), w_gate[:, first:first + H_WIN].astype(jnp.float32).reshape(D, per_expert, shard_width))
        parts = gate_parts + jnp.einsum("rgh,dgh->grd", up_grad.astype(jnp.float32).reshape(row_total, per_expert, shard_width), w_up[:, first:first + H_WIN].astype(jnp.float32).reshape(D, per_expert, shard_width))
        rounded = lax.optimization_barrier(parts.astype(jnp.bfloat16))
        summed = jnp.sum(rounded.astype(jnp.float32), axis=0)
        picked = summed[jnp.minimum(target, row_total - 1)]
        result = result + jnp.sum(jnp.where(hit[:, :, None], picked, jnp.float32(0.0)), axis=1)
    input_grad = result.astype(jnp.bfloat16)
    return input_grad, jnp.concatenate(grads_gate, axis=1), jnp.concatenate(grads_up, axis=1), jnp.concatenate(grads_down, axis=0)


def reference(tokens, out_grad, expert_ids, slot_ids, gate_int, saved_gate, saved_up, w_gate, w_up, w_down):
    input_grads = []
    all_gate = []
    all_up = []
    all_down = []
    for layer_index in range(SECTIONS):
        outcome = section_grads(tokens[layer_index], out_grad[layer_index], expert_ids[layer_index], slot_ids[layer_index], gate_int[layer_index], saved_gate[layer_index], saved_up[layer_index], w_gate[layer_index], w_up[layer_index], w_down[layer_index])
        input_grads.append(outcome[0])
        all_gate.append(outcome[1])
        all_up.append(outcome[2])
        all_down.append(outcome[3])
    arriving = input_grads[1:] + [jnp.zeros((TOKENS, D), jnp.bfloat16)]
    return jnp.stack(arriving), jnp.stack(all_gate), jnp.stack(all_up), jnp.stack(all_down)
```

```python
import functools

import jax
import jax.numpy as jnp
from jax import lax
from jax.experimental import pallas as pl
from jax.experimental.pallas import tpu as pltpu
from jax.sharding import PartitionSpec as P


EXPERTS = 8
E_WIN = 2
BF16 = jnp.bfloat16
F32 = jnp.float32
NT = (((1,), (1,)), ((), ()))
TN = (((0,), (0,)), ((), ()))
NN = (((1,), (0,)), ((), ()))
MIB = 2**20


def vmem():
    return pl.BlockSpec(memory_space=pltpu.VMEM)


def anywhere():
    return pl.BlockSpec(memory_space=pl.ANY)


def hbm():
    return pl.BlockSpec(memory_space=pltpu.HBM)


def smem():
    return pl.BlockSpec(memory_space=pltpu.SMEM)


def piece(total, wanted):
    for size in (wanted, 512, 256, 128):
        if size <= wanted and total % size == 0:
            return size
    return total


def like(shape, dtype=BF16):
    return jax.ShapeDtypeStruct(shape, dtype)


def params(mib):
    return pltpu.CompilerParams(vmem_limit_bytes=int(mib * MIB))


def placement(half, ids, slots, weights, capacity):
    rows = lax.broadcasted_iota(jnp.int32, (2 * capacity, ids.shape[1]), 0)
    matrix = jnp.zeros(rows.shape, F32)
    for k in range(2):
        expert = ids[k : k + 1, :]
        place = jnp.where(expert == half, 0, capacity) + slots[k : k + 1, :]
        hit = jnp.logical_and(rows == place, expert < E_WIN)
        matrix += jnp.where(hit, weights[k : k + 1, :], 0.0)
    return matrix.astype(BF16)


def pick_kernel(capacity, half_ref, *refs):
    sources, outs, copies, sems = refs[:5], refs[5:10], refs[10:15], refs[15]
    half = half_ref[0]
    flying = [
        pltpu.make_async_copy(source, copy, sems.at[n])
        for n, (source, copy) in enumerate(zip(sources, copies))
    ]
    for copy in flying:
        copy.start()
    for copy in flying[:4]:
        copy.wait()
    ids, slots, gates = (copies[n][...] for n in range(3))
    grads_own, grads_far, in_own, in_far, tables = outs
    scaled = placement(half, ids, slots, gates.astype(F32) / 256.0, capacity)
    plain = placement(half, ids, slots, jnp.ones(ids.shape, F32), capacity)
    rows = lax.dot_general(scaled, copies[3][...], NN, preferred_element_type=F32).astype(BF16)
    grads_own[...] = rows[:capacity]
    grads_far[...] = rows[capacity:]
    tables[:2, :] = ids
    tables[2:, :] = slots
    flying[4].wait()
    rows = lax.dot_general(plain, copies[4][...], NN, preferred_element_type=F32).astype(BF16)
    in_own[...] = rows[:capacity]
    in_far[...] = rows[capacity:]


def pick(half, ids, slots, gates, grads, tokens, capacity):
    width = tokens.shape[1]
    sources = (ids, slots, gates, grads, tokens)
    return pl.pallas_call(
        functools.partial(pick_kernel, capacity),
        in_specs=[smem()] + [hbm()] * len(sources),
        out_specs=[vmem()] * 5,
        out_shape=[like((capacity, width))] * 4 + [like((4, ids.shape[1]), jnp.int32)],
        scratch_shapes=[pltpu.VMEM(x.shape, x.dtype) for x in sources]
        + [pltpu.SemaphoreType.DMA((len(sources),))],
        compiler_params=params(8),
        cost_estimate=pl.CostEstimate(
            flops=2**36, bytes_accessed=6 * tokens.size, transcendentals=0
        ),
    )(half, *sources)


def hidden_kernel(capacity, pairs, index_ref, *refs):
    blocks = refs[: len(pairs)]
    gate_hbm, up_hbm, w_down, rows, gate_grad, up_grad, hidden = refs[len(pairs) : len(pairs) + 7]
    gate, up, block_sems, saved_sems = refs[len(pairs) + 7 :]
    landings = land(capacity, pairs, index_ref[0], blocks, rows, block_sems)
    saved = [
        pltpu.make_async_copy(gate_hbm, gate, saved_sems.at[0]),
        pltpu.make_async_copy(up_hbm, up, saved_sems.at[1]),
    ]
    for copy in landings + saved:
        copy.start()
    for copy in landings + saved:
        copy.wait()
    units, step = w_down.shape[0], 256
    for start in range(0, units, step):
        some = slice(start, min(start + step, units))
        grad = lax.dot_general(rows[...], w_down[some, :], NT, preferred_element_type=F32)
        g = gate[:, some].astype(F32)
        u = up[:, some].astype(F32)
        s = jax.nn.sigmoid(g)
        act = g * s
        hidden[:, some] = (act * u).astype(BF16)
        gate_grad[:, some] = (grad * u * s * (1.0 + g * (1.0 - s))).astype(BF16)
        up_grad[:, some] = (grad * act).astype(BF16)


def hidden_stage(index, blocks, pairs, gate, up, w_down, capacity):
    units, width = w_down.shape
    total = gate.shape[0]
    return pl.pallas_call(
        functools.partial(hidden_kernel, capacity, pairs),
        in_specs=[smem()] + [anywhere()] * len(blocks) + [hbm()] * 2 + [vmem()],
        out_specs=[vmem()] * 4,
        out_shape=[like((total, width))] + [like((total, units))] * 3,
        scratch_shapes=[
            pltpu.VMEM((total, units), BF16),
            pltpu.VMEM((total, units), BF16),
            pltpu.SemaphoreType.DMA((total // capacity,)),
            pltpu.SemaphoreType.DMA((2,)),
        ],
        compiler_params=params(6),
        cost_estimate=pl.CostEstimate(
            flops=2 * total * units * width, bytes_accessed=2 * units * width, transcendentals=0
        ),
    )(index, *blocks, gate, up, w_down)


def part_kernel(capacity, group, step, index_ref, *refs):
    gate_grad, up_grad, w_gate, w_up = refs[:4]
    outs, stage = refs[4 : 4 + group], refs[4 + group]
    index = index_ref[0]
    for i in range(w_gate.shape[0] // step):
        some = slice(i * step, (i + 1) * step)
        part = lax.dot_general(gate_grad[...], w_gate[some, :], NT, preferred_element_type=F32)
        part += lax.dot_general(up_grad[...], w_up[some, :], NT, preferred_element_type=F32)
        stage[i % 2] = part.astype(BF16)
        for m in range(2 * group):
            source = pl.multiple_of(jnp.bitwise_xor(index, m) * capacity, capacity)
            start = m // group * capacity
            outs[m % group][start : start + capacity, some] = stage[
                i % 2, pl.ds(source, capacity), :
            ]


def part_stage(index, gate_grad, up_grad, w_gate, w_up, capacity, group):
    width, units = w_gate.shape
    total = gate_grad.shape[0]
    step = piece(width, 512)
    return pl.pallas_call(
        functools.partial(part_kernel, capacity, group, step),
        in_specs=[smem()] + [vmem()] * 4,
        out_specs=[vmem()] * group,
        out_shape=[like((2 * capacity, width))] * group,
        scratch_shapes=[pltpu.VMEM((2, total, step), BF16)],
        compiler_params=params(6),
        cost_estimate=pl.CostEstimate(
            flops=4 * total * units * width, bytes_accessed=4 * units * width, transcendentals=0
        ),
    )(index, gate_grad, up_grad, w_gate, w_up)


def land(capacity, pairs, index, blocks, rows, sems):
    copies = []
    for block, members in zip(blocks, pairs):
        for part, m in enumerate(members):
            start = pl.multiple_of(jnp.bitwise_xor(index, m) * capacity, capacity)
            copies.append(
                pltpu.make_async_copy(
                    block.at[pl.ds(part * capacity, capacity)],
                    rows.at[pl.ds(start, capacity)],
                    sems.at[m],
                )
            )
    return copies


def weight_body(step, depth, left, right, out, ring, sems):
    flying = [None] * depth
    for i in range(left.shape[1] // step):
        slot = i % depth
        value = lax.dot_general(
            left[:, i * step : (i + 1) * step], right[...], TN, preferred_element_type=F32
        ).astype(BF16)
        if flying[slot] is not None:
            flying[slot].wait()
        ring[slot] = value
        copy = pltpu.make_async_copy(ring.at[slot], out.at[pl.ds(i * step, step)], sems.at[slot])
        copy.start()
        flying[slot] = copy
    for copy in flying:
        if copy is not None:
            copy.wait()


def landing_kernel(capacity, pairs, step, depth, index_ref, *refs):
    blocks = refs[: len(pairs)]
    right, out, rows, ring, sems, block_sems = refs[len(pairs) :]
    copies = land(capacity, pairs, index_ref[0], blocks, rows, block_sems)
    for copy in copies:
        copy.start()
    for copy in copies:
        copy.wait()
    weight_body(step, depth, rows, right, out, ring, sems)


def weight_sizes(rows, columns, total, wanted):
    step = piece(rows, wanted)
    depth = min(4, rows // step)
    return step, depth, dict(
        compiler_params=params(32),
        cost_estimate=pl.CostEstimate(
            flops=2 * total * rows * columns, bytes_accessed=2 * rows * columns, transcendentals=0
        ),
    )


def weight_stage(left, right, wanted):
    total, rows = left.shape
    columns = right.shape[1]
    step, depth, more = weight_sizes(rows, columns, total, wanted)
    return pl.pallas_call(
        functools.partial(weight_body, step, depth),
        in_specs=[vmem()] * 2,
        out_specs=hbm(),
        out_shape=like((rows, columns)),
        scratch_shapes=[
            pltpu.VMEM((depth, step, columns), BF16),
            pltpu.SemaphoreType.DMA((depth,)),
        ],
        **more,
    )(left, right)


def landing_stage(index, blocks, pairs, right, wanted, capacity):
    total, columns = right.shape
    rows = blocks[0].shape[1]
    step, depth, more = weight_sizes(rows, columns, total, wanted)
    return pl.pallas_call(
        functools.partial(landing_kernel, capacity, pairs, step, depth),
        in_specs=[smem()] + [anywhere()] * len(blocks) + [vmem()],
        out_specs=[hbm(), vmem()],
        out_shape=[like((rows, columns)), like((total, rows))],
        scratch_shapes=[
            pltpu.VMEM((depth, step, columns), BF16),
            pltpu.SemaphoreType.DMA((depth,)),
            pltpu.SemaphoreType.DMA((total // capacity,)),
        ],
        **more,
    )(index, *blocks, right)


def join_kernel(capacity, shares, half_ref, tables, *refs):
    out_ref = refs[-1]
    ones = jnp.ones((2, tables.shape[1]), F32)
    matrix = placement(half_ref[0], tables[:2, :], tables[2:, :], ones, capacity)
    width = out_ref.shape[1] // shares
    for share in range(shares):
        own, far = refs[2 * share : 2 * share + 2]
        total = lax.dot_general(matrix[:capacity], own[...], TN, preferred_element_type=F32)
        total += lax.dot_general(matrix[capacity:], far[...], TN, preferred_element_type=F32)
        out_ref[:, share * width : (share + 1) * width] = total.astype(BF16)


def join(half, tables, pieces, capacity):
    shares = len(pieces) // 2
    return pl.pallas_call(
        functools.partial(join_kernel, capacity, shares),
        in_specs=[smem()] + [vmem()] * (1 + len(pieces)),
        out_specs=vmem(),
        out_shape=like((tables.shape[1], shares * pieces[0].shape[1])),
        compiler_params=params(8),
    )(half, tables, *pieces)


def to_partner(value, m):
    peers = lax.axis_size("expert")
    return lax.ppermute(value, "expert", [(i, i ^ m) for i in range(peers)])


def to_behind(value, m):
    peers, layers = lax.axis_size("expert"), lax.axis_size("section")
    pairs = [
        (s * peers + i, (s - 1) * peers + (i ^ m)) for s in range(1, layers) for i in range(peers)
    ]
    return lax.ppermute(value, ("section", "expert"), pairs)


def shards(
    tokens, out_grad, expert_ids, slot_ids, gate_int, saved_gate, saved_up, w_gate, w_up, w_down
):
    peers = lax.axis_size("expert")
    group = peers // E_WIN
    capacity = tokens.shape[1] * 2 // EXPERTS
    stay = functools.partial(pltpu.with_memory_space_constraint, memory_space=pltpu.HBM)
    place = lax.axis_index("expert").astype(jnp.int32)
    index = place.reshape(1)
    half = (place // group).reshape(1)
    shares = 1

    grads_own, grads_far, in_own, in_far, tables = pick(
        half,
        stay(expert_ids[0].T),
        stay(slot_ids[0].T),
        stay(gate_int[0].T),
        stay(out_grad[0]),
        stay(tokens[0]),
        capacity,
    )
    crossed = to_partner(grads_far, group)
    near = [grads_own] + [to_partner(grads_own, m) for m in range(1, group)]
    tables = to_behind(tables, 0)
    far = [crossed] + [to_partner(crossed, m) for m in range(1, group)]
    in_crossed = to_partner(in_far, group)
    singles = [(m,) for m in range(2 * group)]
    rows_grad, gate_grad, up_grad, hidden = hidden_stage(
        index,
        near + far,
        singles,
        stay(saved_gate[0]),
        stay(saved_up[0]),
        w_down[0],
        capacity,
    )
    both = jnp.concatenate([in_own, in_crossed], axis=0)
    in_blocks = [both] + [to_partner(both, m) for m in range(1, group)]
    parts, returned = [], []
    for share in range(shares):
        parts.append(
            part_stage(
                index,
                gate_grad,
                up_grad,
                w_gate[0],
                w_up[0],
                capacity,
                group,
            )
        )
        returned.append([to_partner(parts[share][m], m) for m in range(1, group)])
    grad_down = weight_stage(hidden, rows_grad, 256)
    pieces = []
    for share in range(shares):
        summed = parts[share][0].astype(F32)
        for part in returned[share]:
            summed += part.astype(F32)
        summed = summed.astype(BF16)
        kept, sent = summed[:capacity], summed[capacity:]
        sent = to_behind(sent, group)
        kept = to_behind(kept, 0)
        pieces += [kept, sent]
    pairs = [(m, m + group) for m in range(group)]
    grad_gate, rows_in = landing_stage(index, in_blocks, pairs, gate_grad, 512, capacity)
    grad_up = weight_stage(rows_in, up_grad, 512)
    arriving = join(half, tables, pieces, capacity)
    return (arriving[None], grad_gate[None], grad_up[None], grad_down[None])


def solution(mesh):
    rows = P("section", "expert", None)
    columns = P("section", None, "expert")
    return jax.shard_map(
        shards,
        mesh=mesh,
        in_specs=(rows,) * 5 + (columns,) * 4 + (rows,),
        out_specs=(rows, columns, columns, rows),
        check_vma=False,
    )
```

```python
import functools

import jax
import jax.numpy as jnp
from jax import lax
from jax.experimental import pallas as pl
from jax.experimental.pallas import tpu as pltpu
from jax.sharding import PartitionSpec as P


EXPERTS = 8
E_WIN = 2
BF16 = jnp.bfloat16
F32 = jnp.float32
NT = (((1,), (1,)), ((), ()))
TN = (((0,), (0,)), ((), ()))
NN = (((1,), (0,)), ((), ()))
MIB = 2**20


def vmem():
    return pl.BlockSpec(memory_space=pltpu.VMEM)


def anywhere():
    return pl.BlockSpec(memory_space=pl.ANY)


def hbm():
    return pl.BlockSpec(memory_space=pltpu.HBM)


def smem():
    return pl.BlockSpec(memory_space=pltpu.SMEM)


def piece(total, wanted):
    for size in (wanted, 512, 256, 128):
        if size <= wanted and total % size == 0:
            return size
    return total


def like(shape, dtype=BF16):
    return jax.ShapeDtypeStruct(shape, dtype)


def params(mib):
    return pltpu.CompilerParams(vmem_limit_bytes=int(mib * MIB))


def placement(half, ids, slots, weights, capacity):
    rows = lax.broadcasted_iota(jnp.int32, (2 * capacity, ids.shape[1]), 0)
    matrix = jnp.zeros(rows.shape, F32)
    for k in range(2):
        expert = ids[k : k + 1, :]
        place = jnp.where(expert == half, 0, capacity) + slots[k : k + 1, :]
        hit = jnp.logical_and(rows == place, expert < E_WIN)
        matrix += jnp.where(hit, weights[k : k + 1, :], 0.0)
    return matrix.astype(BF16)


def pick_kernel(capacity, half_ref, *refs):
    sources, outs, copies, sems = refs[:5], refs[5:10], refs[10:15], refs[15]
    half = half_ref[0]
    flying = [
        pltpu.make_async_copy(source, copy, sems.at[n])
        for n, (source, copy) in enumerate(zip(sources, copies))
    ]
    for copy in flying:
        copy.start()
    for copy in flying[:4]:
        copy.wait()
    ids, slots, gates = (copies[n][...] for n in range(3))
    grads_own, grads_far, in_own, in_far, picks = outs
    scaled = placement(half, ids, slots, gates.astype(F32) / 256.0, capacity)
    plain = placement(half, ids, slots, jnp.ones(ids.shape, F32), capacity)
    rows = lax.dot_general(scaled, copies[3][...], NN, preferred_element_type=F32).astype(BF16)
    grads_own[...] = rows[:capacity]
    grads_far[...] = rows[capacity:]
    picks[...] = jnp.concatenate([plain[:capacity], plain[capacity:]], axis=1)
    flying[4].wait()
    rows = lax.dot_general(plain, copies[4][...], NN, preferred_element_type=F32).astype(BF16)
    in_own[...] = rows[:capacity]
    in_far[...] = rows[capacity:]


def pick(half, ids, slots, gates, grads, tokens, capacity):
    width = tokens.shape[1]
    sources = (ids, slots, gates, grads, tokens)
    return pl.pallas_call(
        functools.partial(pick_kernel, capacity),
        in_specs=[smem()] + [hbm()] * len(sources),
        out_specs=[vmem()] * 5,
        out_shape=[like((capacity, width))] * 4 + [like((capacity, 2 * ids.shape[1]))],
        scratch_shapes=[pltpu.VMEM(x.shape, x.dtype) for x in sources]
        + [pltpu.SemaphoreType.DMA((len(sources),))],
        compiler_params=params(8),
        cost_estimate=pl.CostEstimate(
            flops=2**36, bytes_accessed=6 * tokens.size, transcendentals=0
        ),
    )(half, *sources)


def saved_kernel(gate_hbm, up_hbm, hidden, act_ref, slope_ref, gate, up, sems):
    copies = [
        pltpu.make_async_copy(gate_hbm, gate, sems.at[0]),
        pltpu.make_async_copy(up_hbm, up, sems.at[1]),
    ]
    for copy in copies:
        copy.start()
    for copy in copies:
        copy.wait()
    g = gate[...].astype(F32)
    u = up[...].astype(F32)
    s = jax.nn.sigmoid(g)
    act = g * s
    hidden[...] = (act * u).astype(BF16)
    act_ref[...] = act
    slope_ref[...] = u * s * (1.0 + g * (1.0 - s))


def saved_stage(gate, up):
    shape = gate.shape
    return pl.pallas_call(
        saved_kernel,
        in_specs=[hbm()] * 2,
        out_specs=[vmem()] * 3,
        out_shape=[like(shape), like(shape, F32), like(shape, F32)],
        scratch_shapes=[pltpu.VMEM(shape, BF16)] * 2 + [pltpu.SemaphoreType.DMA((2,))],
        compiler_params=params(4),
        cost_estimate=pl.CostEstimate(
            flops=16 * gate.size, bytes_accessed=14 * gate.size, transcendentals=gate.size
        ),
    )(gate, up)


def hidden_kernel(capacity, pairs, index_ref, *refs):
    blocks = refs[: len(pairs)]
    act, slope, w_down, rows, gate_grad, up_grad, block_sems = refs[len(pairs) :]
    landings = land(capacity, pairs, index_ref[0], blocks, rows, block_sems)
    for copy in landings:
        copy.start()
    for copy in landings:
        copy.wait()
    units, step = w_down.shape[0], 256
    for start in range(0, units, step):
        some = slice(start, min(start + step, units))
        grad = lax.dot_general(w_down[some, :], rows[...], NT, preferred_element_type=F32).T
        gate_grad[:, some] = (grad * slope[:, some]).astype(BF16)
        up_grad[:, some] = (grad * act[:, some]).astype(BF16)


def hidden_stage(index, blocks, pairs, act, slope, w_down, capacity):
    units, width = w_down.shape
    total = act.shape[0]
    return pl.pallas_call(
        functools.partial(hidden_kernel, capacity, pairs),
        in_specs=[smem()] + [anywhere()] * len(blocks) + [vmem()] * 3,
        out_specs=[vmem()] * 3,
        out_shape=[like((total, width))] + [like((total, units))] * 2,
        scratch_shapes=[pltpu.SemaphoreType.DMA((total // capacity,))],
        compiler_params=params(6),
        cost_estimate=pl.CostEstimate(
            flops=2 * total * units * width, bytes_accessed=2 * units * width, transcendentals=0
        ),
    )(index, *blocks, act, slope, w_down)


def part_kernel(capacity, group, step, index_ref, *refs):
    gate_grad, up_grad, w_gate, up_hbm = refs[:4]
    outs = refs[4 : 4 + group]
    half, stage, w_up, sems = refs[4 + group :]
    index = index_ref[0]
    cuts = sems.shape[0]
    width = w_gate.shape[0]
    size = width // cuts
    ahead = [
        pltpu.make_async_copy(
            up_hbm.at[pl.ds(n * size, size)], w_up.at[pl.ds(n * size, size)], sems.at[n]
        )
        for n in range(cuts)
    ]
    for copy in ahead:
        copy.start()
    for start in range(0, width, step):
        some = slice(start, start + step)
        half[some, :] = lax.dot_general(
            w_gate[some, :], gate_grad[...], NT, preferred_element_type=F32
        )
    for n in range(cuts):
        ahead[n].wait()
        for start in range(n * size, (n + 1) * size, min(step, size)):
            some = slice(start, start + min(step, size))
            part = half[some, :] + lax.dot_general(
                w_up[some, :], up_grad[...], NT, preferred_element_type=F32
            )
            stage[:, some] = part.T.astype(BF16)
    for m in range(2 * group):
        source = pl.multiple_of(jnp.bitwise_xor(index, m) * capacity, capacity)
        start = m // group * capacity
        outs[m % group][start : start + capacity, :] = stage[pl.ds(source, capacity), :]


def part_stage(index, gate_grad, up_grad, w_gate, w_up, capacity, group):
    width, units = w_gate.shape
    total = gate_grad.shape[0]
    step = piece(width, 512)
    return pl.pallas_call(
        functools.partial(part_kernel, capacity, group, step),
        in_specs=[smem()] + [vmem()] * 3 + [hbm()],
        out_specs=[vmem()] * group,
        out_shape=[like((2 * capacity, width))] * group,
        scratch_shapes=[
            pltpu.VMEM((width, total), F32),
            pltpu.VMEM((total, width), BF16),
            pltpu.VMEM((width, units), BF16),
            pltpu.SemaphoreType.DMA((4,)),
        ],
        compiler_params=params(24),
        cost_estimate=pl.CostEstimate(
            flops=4 * total * units * width, bytes_accessed=4 * units * width, transcendentals=0
        ),
    )(index, gate_grad, up_grad, w_gate, w_up)


def land(capacity, pairs, index, blocks, rows, sems):
    copies = []
    for block, members in zip(blocks, pairs):
        for part, m in enumerate(members):
            start = pl.multiple_of(jnp.bitwise_xor(index, m) * capacity, capacity)
            copies.append(
                pltpu.make_async_copy(
                    block.at[pl.ds(part * capacity, capacity)],
                    rows.at[pl.ds(start, capacity)],
                    sems.at[m],
                )
            )
    return copies


def write_out(left, right, out, stage, sems):
    step = out.shape[0] // sems.shape[0]
    copies = []
    for n in range(sems.shape[0]):
        some = slice(n * step, (n + 1) * step)
        stage[some, :] = lax.dot_general(
            left[:, some], right[...], TN, preferred_element_type=F32
        ).astype(BF16)
        copy = pltpu.make_async_copy(
            stage.at[pl.ds(n * step, step)], out.at[pl.ds(n * step, step)], sems.at[n]
        )
        copy.start()
        copies.append(copy)
    return copies


def first_kernel(capacity, pairs, index_ref, *refs):
    blocks = refs[: len(pairs)]
    hidden, rows_grad, gate_grad, down, gate, rows_in = refs[len(pairs) : len(pairs) + 6]
    stage_down, stage_gate, sems_down, sems_gate, block_sems = refs[len(pairs) + 6 :]
    copies = land(capacity, pairs, index_ref[0], blocks, rows_in, block_sems)
    for copy in copies:
        copy.start()
    left = write_out(hidden, rows_grad, down, stage_down, sems_down)
    for copy in copies:
        copy.wait()
    left += write_out(rows_in, gate_grad, gate, stage_gate, sems_gate)
    for copy in left:
        copy.wait()


def weight_cost(count, total, units, width):
    return pl.CostEstimate(
        flops=2 * count * total * units * width,
        bytes_accessed=2 * count * units * width,
        transcendentals=0,
    )


def first_stage(index, blocks, pairs, hidden, rows_grad, gate_grad, capacity):
    total, units = hidden.shape
    width = rows_grad.shape[1]
    return pl.pallas_call(
        functools.partial(first_kernel, capacity, pairs),
        in_specs=[smem()] + [anywhere()] * len(blocks) + [vmem()] * 3,
        out_specs=[hbm(), hbm(), vmem()],
        out_shape=[like((units, width)), like((width, units)), like((total, width))],
        scratch_shapes=[
            pltpu.VMEM((units, width), BF16),
            pltpu.VMEM((width, units), BF16),
            pltpu.SemaphoreType.DMA((units // piece(units, 256),)),
            pltpu.SemaphoreType.DMA((width // piece(width, 512),)),
            pltpu.SemaphoreType.DMA((total // capacity,)),
        ],
        compiler_params=params(36),
        cost_estimate=weight_cost(2, total, units, width),
    )(index, *blocks, hidden, rows_grad, gate_grad)


def second_kernel(left, right, out, stage, sems):
    for copy in write_out(left, right, out, stage, sems):
        copy.wait()


def second_stage(rows_in, up_grad):
    total, width = rows_in.shape
    units = up_grad.shape[1]
    return pl.pallas_call(
        second_kernel,
        in_specs=[vmem()] * 2,
        out_specs=hbm(),
        out_shape=like((width, units)),
        scratch_shapes=[
            pltpu.VMEM((width, units), BF16),
            pltpu.SemaphoreType.DMA((width // piece(width, 256),)),
        ],
        compiler_params=params(24),
        cost_estimate=weight_cost(1, total, units, width),
    )(rows_in, up_grad)


def join_kernel(kept_ref, sent_ref, out_ref):
    tokens, width = out_ref.shape
    picks = kept_ref[:, width:]
    total = lax.dot_general(
        picks[:, :tokens], kept_ref[:, :width], TN, preferred_element_type=F32
    )
    total += lax.dot_general(
        picks[:, tokens : 2 * tokens], sent_ref[...], TN, preferred_element_type=F32
    )
    out_ref[...] = total.astype(BF16)


def join(kept, sent, tokens):
    return pl.pallas_call(
        join_kernel,
        in_specs=[vmem()] * 2,
        out_specs=vmem(),
        out_shape=like((tokens, sent.shape[1])),
        compiler_params=params(8),
    )(kept, sent)


def to_partner(value, m):
    peers = lax.axis_size("expert")
    return lax.ppermute(value, "expert", [(i, i ^ m) for i in range(peers)])


def to_behind(value, m):
    peers, layers = lax.axis_size("expert"), lax.axis_size("section")
    pairs = [
        (s * peers + i, (s - 1) * peers + (i ^ m)) for s in range(1, layers) for i in range(peers)
    ]
    return lax.ppermute(value, ("section", "expert"), pairs)


def shards(
    tokens, out_grad, expert_ids, slot_ids, gate_int, saved_gate, saved_up, w_gate, w_up, w_down
):
    peers = lax.axis_size("expert")
    group = peers // E_WIN
    capacity = tokens.shape[1] * 2 // EXPERTS
    stay = functools.partial(pltpu.with_memory_space_constraint, memory_space=pltpu.HBM)
    place = lax.axis_index("expert").astype(jnp.int32)
    index = place.reshape(1)
    half = (place // group).reshape(1)

    grads_own, grads_far, in_own, in_far, picks = pick(
        half,
        stay(expert_ids[0].T),
        stay(slot_ids[0].T),
        stay(gate_int[0].T),
        stay(out_grad[0]),
        stay(tokens[0]),
        capacity,
    )
    crossed = to_partner(grads_far, group)
    near = [grads_own] + [to_partner(grads_own, m) for m in range(1, group)]
    far = [crossed] + [to_partner(crossed, m) for m in range(1, group)]
    in_crossed = to_partner(in_far, group)
    hidden, act, slope = saved_stage(stay(saved_gate[0]), stay(saved_up[0]))
    singles = [(m,) for m in range(2 * group)]
    rows_grad, gate_grad, up_grad = hidden_stage(
        index,
        near + far,
        singles,
        act,
        slope,
        w_down[0],
        capacity,
    )
    both = jnp.concatenate([in_own, in_crossed], axis=0)
    in_blocks = [both] + [to_partner(both, m) for m in range(1, group)]
    parts = part_stage(
        index, gate_grad, up_grad, w_gate[0], stay(w_up[0]), capacity, group
    )
    returned = [to_partner(parts[m], m) for m in range(1, group)]
    pairs = [(m, m + group) for m in range(group)]
    grad_down, grad_gate, rows_in = first_stage(
        index, in_blocks, pairs, hidden, rows_grad, gate_grad, capacity
    )
    summed = parts[0].astype(F32)
    for part in returned:
        summed += part.astype(F32)
    summed = summed.astype(BF16)
    kept = jnp.concatenate([summed[:capacity], picks], axis=1)
    sent = summed[capacity:]
    sent = to_behind(sent, group)
    kept = to_behind(kept, 0)
    grad_up = second_stage(rows_in, up_grad)
    arriving = join(kept, sent, tokens.shape[1])
    return (arriving[None], grad_gate[None], grad_up[None], grad_down[None])


def solution(mesh):
    rows = P("section", "expert", None)
    columns = P("section", None, "expert")
    return jax.shard_map(
        shards,
        mesh=mesh,
        in_specs=(rows,) * 5 + (columns,) * 4 + (rows,),
        out_specs=(rows, columns, columns, rows),
        check_vma=False,
    )
```

```python
import functools

import jax
import jax.numpy as jnp
from jax import lax
from jax.experimental import pallas as pl
from jax.experimental.pallas import tpu as pltpu
from jax.sharding import PartitionSpec as P


EXPERTS = 8
E_WIN = 2
EARLY = 2
GRANT = 24
BF16 = jnp.bfloat16
F32 = jnp.float32
NT = (((1,), (1,)), ((), ()))
TN = (((0,), (0,)), ((), ()))
NN = (((1,), (0,)), ((), ()))
MIB = 2**20


def vmem():
    return pl.BlockSpec(memory_space=pltpu.VMEM)


def anywhere():
    return pl.BlockSpec(memory_space=pl.ANY)


def hbm():
    return pl.BlockSpec(memory_space=pltpu.HBM)


def smem():
    return pl.BlockSpec(memory_space=pltpu.SMEM)


def piece(total, wanted):
    for size in (wanted, 512, 256, 128):
        if size <= wanted and total % size == 0:
            return size
    return total


def like(shape, dtype=BF16):
    return jax.ShapeDtypeStruct(shape, dtype)


def params(mib):
    return pltpu.CompilerParams(vmem_limit_bytes=int(mib * MIB))


def placement(half, ids, slots, weights, capacity):
    rows = lax.broadcasted_iota(jnp.int32, (2 * capacity, ids.shape[1]), 0)
    matrix = jnp.zeros(rows.shape, F32)
    for k in range(2):
        expert = ids[k : k + 1, :]
        place = jnp.where(expert == half, 0, capacity) + slots[k : k + 1, :]
        hit = jnp.logical_and(rows == place, expert < E_WIN)
        matrix += jnp.where(hit, weights[k : k + 1, :], 0.0)
    return matrix.astype(BF16)


def pick_kernel(capacity, half_ref, *refs):
    sources, outs, copies, sems = refs[:5], refs[5:10], refs[10:15], refs[15]
    half = half_ref[0]
    flying = [
        pltpu.make_async_copy(source, copy, sems.at[n])
        for n, (source, copy) in enumerate(zip(sources, copies))
    ]
    for copy in flying:
        copy.start()
    for copy in flying[:4]:
        copy.wait()
    ids, slots, gates = (copies[n][...] for n in range(3))
    grads_own, grads_far, in_own, in_far, picks = outs
    scaled = placement(half, ids, slots, gates.astype(F32) / 256.0, capacity)
    plain = placement(half, ids, slots, jnp.ones(ids.shape, F32), capacity)
    rows = lax.dot_general(scaled, copies[3][...], NN, preferred_element_type=F32).astype(BF16)
    grads_own[...] = rows[:capacity]
    grads_far[...] = rows[capacity:]
    picks[...] = jnp.concatenate([plain[:capacity], plain[capacity:]], axis=1)
    flying[4].wait()
    rows = lax.dot_general(plain, copies[4][...], NN, preferred_element_type=F32).astype(BF16)
    in_own[...] = rows[:capacity]
    in_far[...] = rows[capacity:]


def pick(half, ids, slots, gates, grads, tokens, capacity):
    width = tokens.shape[1]
    sources = (ids, slots, gates, grads, tokens)
    return pl.pallas_call(
        functools.partial(pick_kernel, capacity),
        in_specs=[smem()] + [hbm()] * len(sources),
        out_specs=[vmem()] * 5,
        out_shape=[like((capacity, width))] * 4 + [like((capacity, 2 * ids.shape[1]))],
        scratch_shapes=[pltpu.VMEM(x.shape, x.dtype) for x in sources]
        + [pltpu.SemaphoreType.DMA((len(sources),))],
        compiler_params=params(8),
        cost_estimate=pl.CostEstimate(
            flops=2**36, bytes_accessed=6 * tokens.size, transcendentals=0
        ),
    )(half, *sources)


def saved_kernel(gate_hbm, up_hbm, hidden, act_ref, slope_ref, gate, up, sems):
    copies = [
        pltpu.make_async_copy(gate_hbm, gate, sems.at[0]),
        pltpu.make_async_copy(up_hbm, up, sems.at[1]),
    ]
    for copy in copies:
        copy.start()
    for copy in copies:
        copy.wait()
    g = gate[...].astype(F32)
    u = up[...].astype(F32)
    s = jax.nn.sigmoid(g)
    act = g * s
    hidden[...] = (act * u).astype(BF16)
    act_ref[...] = act
    slope_ref[...] = u * s * (1.0 + g * (1.0 - s))


def saved_stage(gate, up):
    shape = gate.shape
    return pl.pallas_call(
        saved_kernel,
        in_specs=[hbm()] * 2,
        out_specs=[vmem()] * 3,
        out_shape=[like(shape), like(shape, F32), like(shape, F32)],
        scratch_shapes=[pltpu.VMEM(shape, BF16)] * 2 + [pltpu.SemaphoreType.DMA((2,))],
        compiler_params=params(4),
        cost_estimate=pl.CostEstimate(
            flops=16 * gate.size, bytes_accessed=14 * gate.size, transcendentals=gate.size
        ),
    )(gate, up)


def hidden_kernel(capacity, pairs, index_ref, *refs):
    blocks = refs[: len(pairs)]
    act, slope, w_down, rows, gate_grad, up_grad, block_sems = refs[len(pairs) :]
    landings = land(capacity, pairs, index_ref[0], blocks, rows, block_sems)
    for copy in landings:
        copy.start()
    for copy in landings:
        copy.wait()
    units, step = w_down.shape[0], 256
    for start in range(0, units, step):
        some = slice(start, min(start + step, units))
        grad = lax.dot_general(w_down[some, :], rows[...], NT, preferred_element_type=F32).T
        gate_grad[:, some] = (grad * slope[:, some]).astype(BF16)
        up_grad[:, some] = (grad * act[:, some]).astype(BF16)


def hidden_stage(index, blocks, pairs, act, slope, w_down, capacity):
    units, width = w_down.shape
    total = act.shape[0]
    return pl.pallas_call(
        functools.partial(hidden_kernel, capacity, pairs),
        in_specs=[smem()] + [anywhere()] * len(blocks) + [vmem()] * 3,
        out_specs=[vmem()] * 3,
        out_shape=[like((total, width))] + [like((total, units))] * 2,
        scratch_shapes=[pltpu.SemaphoreType.DMA((total // capacity,))],
        compiler_params=params(6),
        cost_estimate=pl.CostEstimate(
            flops=2 * total * units * width, bytes_accessed=2 * units * width, transcendentals=0
        ),
    )(index, *blocks, act, slope, w_down)


def part_kernel(capacity, group, step, early, index_ref, *refs):
    gate_grad, up_grad, w_gate, hidden, rows_grad, up_hbm = refs[:6]
    outs, down = refs[6 : 6 + group], refs[6 + group]
    half, stage, w_up, sems, stage_down, sems_down = refs[7 + group :]
    index = index_ref[0]
    cuts = sems.shape[0]
    width = w_gate.shape[0]
    size = width // cuts
    ahead = [
        pltpu.make_async_copy(
            up_hbm.at[pl.ds(n * size, size)], w_up.at[pl.ds(n * size, size)], sems.at[n]
        )
        for n in range(cuts)
    ]
    for copy in ahead:
        copy.start()
    leaving = write_out(hidden, rows_grad, down, stage_down, sems_down, 0, early)
    for start in range(0, width, step):
        some = slice(start, start + step)
        half[some, :] = lax.dot_general(
            w_gate[some, :], gate_grad[...], NT, preferred_element_type=F32
        )
    for n in range(cuts):
        ahead[n].wait()
        for start in range(n * size, (n + 1) * size, min(step, size)):
            some = slice(start, start + min(step, size))
            part = half[some, :] + lax.dot_general(
                w_up[some, :], up_grad[...], NT, preferred_element_type=F32
            )
            stage[:, some] = part.T.astype(BF16)
    for m in range(2 * group):
        source = pl.multiple_of(jnp.bitwise_xor(index, m) * capacity, capacity)
        start = m // group * capacity
        outs[m % group][start : start + capacity, :] = stage[pl.ds(source, capacity), :]
    for copy in leaving:
        copy.wait()


def down_slabs(units):
    slab = piece(units, 256)
    return slab, EARLY * (units // slab) // 7


def part_stage(index, gate_grad, up_grad, w_gate, hidden, rows_grad, w_up, capacity, group):
    width, units = w_gate.shape
    total = gate_grad.shape[0]
    step = piece(width, 512)
    slab, early = down_slabs(units)
    return pl.pallas_call(
        functools.partial(part_kernel, capacity, group, step, early),
        in_specs=[smem()] + [vmem()] * 5 + [hbm()],
        out_specs=[vmem()] * group + [hbm()],
        out_shape=[like((2 * capacity, width))] * group + [like((units, width))],
        scratch_shapes=[
            pltpu.VMEM((width, total), F32),
            pltpu.VMEM((total, width), BF16),
            pltpu.VMEM((width, units), BF16),
            pltpu.SemaphoreType.DMA((4,)),
            pltpu.VMEM((max(early, 1) * slab, width), BF16),
            pltpu.SemaphoreType.DMA((max(early, 1),)),
        ],
        compiler_params=params(GRANT),
        cost_estimate=pl.CostEstimate(
            flops=4 * total * units * width, bytes_accessed=4 * units * width, transcendentals=0
        ),
    )(index, gate_grad, up_grad, w_gate, hidden, rows_grad, w_up)


def land(capacity, pairs, index, blocks, rows, sems):
    copies = []
    for block, members in zip(blocks, pairs):
        for part, m in enumerate(members):
            start = pl.multiple_of(jnp.bitwise_xor(index, m) * capacity, capacity)
            copies.append(
                pltpu.make_async_copy(
                    block.at[pl.ds(part * capacity, capacity)],
                    rows.at[pl.ds(start, capacity)],
                    sems.at[m],
                )
            )
    return copies


def write_out(left, right, out, stage, sems, first=0, count=None):
    count = sems.shape[0] if count is None else count
    step = stage.shape[0] // max(count, 1)
    copies = []
    for n in range(count):
        some = slice(first + n * step, first + (n + 1) * step)
        stage[n * step : (n + 1) * step, :] = lax.dot_general(
            left[:, some], right[...], TN, preferred_element_type=F32
        ).astype(BF16)
        copy = pltpu.make_async_copy(
            stage.at[pl.ds(n * step, step)], out.at[pl.ds(first + n * step, step)], sems.at[n]
        )
        copy.start()
        copies.append(copy)
    return copies


def first_kernel(capacity, pairs, index_ref, *refs):
    blocks = refs[: len(pairs)]
    hidden, rows_grad, gate_grad, _, down, gate, rows_in = refs[len(pairs) : len(pairs) + 7]
    stage_down, stage_gate, sems_down, sems_gate, block_sems = refs[len(pairs) + 7 :]
    begun = down.shape[0] - stage_down.shape[0]
    copies = land(capacity, pairs, index_ref[0], blocks, rows_in, block_sems)
    for copy in copies:
        copy.start()
    left = write_out(hidden, rows_grad, down, stage_down, sems_down, begun)
    for copy in copies:
        copy.wait()
    left += write_out(rows_in, gate_grad, gate, stage_gate, sems_gate)
    for copy in left:
        copy.wait()


def weight_cost(count, total, units, width):
    return pl.CostEstimate(
        flops=2 * count * total * units * width,
        bytes_accessed=2 * count * units * width,
        transcendentals=0,
    )


def first_stage(index, blocks, pairs, hidden, rows_grad, gate_grad, down, capacity):
    total, units = hidden.shape
    width = rows_grad.shape[1]
    slab, early = down_slabs(units)
    late = units // slab - early
    return pl.pallas_call(
        functools.partial(first_kernel, capacity, pairs),
        in_specs=[smem()] + [anywhere()] * len(blocks) + [vmem()] * 3 + [hbm()],
        out_specs=[hbm(), hbm(), vmem()],
        out_shape=[like((units, width)), like((width, units)), like((total, width))],
        scratch_shapes=[
            pltpu.VMEM((late * slab, width), BF16),
            pltpu.VMEM((width, units), BF16),
            pltpu.SemaphoreType.DMA((late,)),
            pltpu.SemaphoreType.DMA((width // piece(width, 512),)),
            pltpu.SemaphoreType.DMA((total // capacity,)),
        ],
        input_output_aliases={4 + len(blocks): 0},
        compiler_params=params(36),
        cost_estimate=weight_cost(2, total, units, width),
    )(index, *blocks, hidden, rows_grad, gate_grad, down)


def second_kernel(left, right, out, stage, sems):
    for copy in write_out(left, right, out, stage, sems):
        copy.wait()


def second_stage(rows_in, up_grad):
    total, width = rows_in.shape
    units = up_grad.shape[1]
    return pl.pallas_call(
        second_kernel,
        in_specs=[vmem()] * 2,
        out_specs=hbm(),
        out_shape=like((width, units)),
        scratch_shapes=[
            pltpu.VMEM((width, units), BF16),
            pltpu.SemaphoreType.DMA((width // piece(width, 256),)),
        ],
        compiler_params=params(24),
        cost_estimate=weight_cost(1, total, units, width),
    )(rows_in, up_grad)


def join_kernel(kept_ref, sent_ref, out_ref):
    tokens, width = out_ref.shape
    picks = kept_ref[:, width:]
    total = lax.dot_general(
        picks[:, :tokens], kept_ref[:, :width], TN, preferred_element_type=F32
    )
    total += lax.dot_general(
        picks[:, tokens : 2 * tokens], sent_ref[...], TN, preferred_element_type=F32
    )
    out_ref[...] = total.astype(BF16)


def join(kept, sent, tokens):
    return pl.pallas_call(
        join_kernel,
        in_specs=[vmem()] * 2,
        out_specs=vmem(),
        out_shape=like((tokens, sent.shape[1])),
        compiler_params=params(8),
    )(kept, sent)


def to_partner(value, m):
    peers = lax.axis_size("expert")
    return lax.ppermute(value, "expert", [(i, i ^ m) for i in range(peers)])


def to_behind(value, m):
    peers, layers = lax.axis_size("expert"), lax.axis_size("section")
    pairs = [
        (s * peers + i, (s - 1) * peers + (i ^ m)) for s in range(1, layers) for i in range(peers)
    ]
    return lax.ppermute(value, ("section", "expert"), pairs)


def shards(
    tokens, out_grad, expert_ids, slot_ids, gate_int, saved_gate, saved_up, w_gate, w_up, w_down
):
    peers = lax.axis_size("expert")
    group = peers // E_WIN
    capacity = tokens.shape[1] * 2 // EXPERTS
    stay = functools.partial(pltpu.with_memory_space_constraint, memory_space=pltpu.HBM)
    place = lax.axis_index("expert").astype(jnp.int32)
    index = place.reshape(1)
    half = (place // group).reshape(1)

    grads_own, grads_far, in_own, in_far, picks = pick(
        half,
        stay(expert_ids[0].T),
        stay(slot_ids[0].T),
        stay(gate_int[0].T),
        stay(out_grad[0]),
        stay(tokens[0]),
        capacity,
    )
    crossed = to_partner(grads_far, group)
    near = [grads_own] + [to_partner(grads_own, m) for m in range(1, group)]
    far = [crossed] + [to_partner(crossed, m) for m in range(1, group)]
    in_crossed = to_partner(in_far, group)
    hidden, act, slope = saved_stage(stay(saved_gate[0]), stay(saved_up[0]))
    singles = [(m,) for m in range(2 * group)]
    rows_grad, gate_grad, up_grad = hidden_stage(
        index,
        near + far,
        singles,
        act,
        slope,
        w_down[0],
        capacity,
    )
    both = jnp.concatenate([in_own, in_crossed], axis=0)
    in_blocks = [both] + [to_partner(both, m) for m in range(1, group)]
    *parts, grad_down = part_stage(
        index,
        gate_grad,
        up_grad,
        w_gate[0],
        hidden,
        rows_grad,
        stay(w_up[0]),
        capacity,
        group,
    )
    returned = [to_partner(parts[m], m) for m in range(1, group)]
    pairs = [(m, m + group) for m in range(group)]
    grad_down, grad_gate, rows_in = first_stage(
        index, in_blocks, pairs, hidden, rows_grad, gate_grad, grad_down, capacity
    )
    summed = parts[0].astype(F32)
    for part in returned:
        summed += part.astype(F32)
    summed = summed.astype(BF16)
    kept = jnp.concatenate([summed[:capacity], picks], axis=1)
    sent = summed[capacity:]
    sent = to_behind(sent, group)
    kept = to_behind(kept, 0)
    grad_up = second_stage(rows_in, up_grad)
    arriving = join(kept, sent, tokens.shape[1])
    return (arriving[None], grad_gate[None], grad_up[None], grad_down[None])


def solution(mesh):
    rows = P("section", "expert", None)
    columns = P("section", None, "expert")
    return jax.shard_map(
        shards,
        mesh=mesh,
        in_specs=(rows,) * 5 + (columns,) * 4 + (rows,),
        out_specs=(rows, columns, columns, rows),
        check_vma=False,
    )
```
